32 devices in a mesh: dp: 16 (over z, x, core), seq: 2 (over y).
Axes of the slice: x: 2, y: 2, z: 4, core: 2. Of those that a mesh axis runs over, the one named last changes fastest.
Arguments:
- tokens: float32 [32, 1024, 768], P('dp', 'seq'), may hold values from -6 to 6
- segments: int32 [32, 1024], P('dp'), may hold values from 0 to 3, never falling along the last dimension, each value on 1 to 512 neighbouring positions
- padding: int32 [32, 1024], P('dp'), may hold values 0 or 1
- query_weight: bfloat16 [768, 768], P(('dp', 'seq')), may hold values from -0.3125 to 0.3125
- query_bias: bfloat16 [768], P(('dp', 'seq')), may hold values from -1.25 to 1.25
- key_weight: bfloat16 [768, 768], P(('dp', 'seq')), may hold values from -0.3125 to 0.3125
- value_weight: bfloat16 [768, 768], P(('dp', 'seq')), may hold values from -0.21875 to 0.21875
- value_bias: bfloat16 [768], P(('dp', 'seq')), may hold values from -1.25 to 1.25
- output_weight: bfloat16 [768, 768], P(('dp', 'seq')), may hold values from -0.875 to 0.875
- output_bias: bfloat16 [768], P(('dp', 'seq')), may hold values from -1.25 to 1.25
- first_gain: bfloat16 [768], P(('dp', 'seq')), may hold values from 0.5 to 1.5
- first_shift: bfloat16 [768], P(('dp', 'seq')), may hold values from -1.25 to 1.25
- inner_weight: bfloat16 [768, 3072], P(('dp', 'seq')), may hold values from -0.21875 to 0.21875
- inner_bias: bfloat16 [3072], P(('dp', 'seq')), may hold values from -1.25 to 1.25
- outer_weight: bfloat16 [3072, 768], P(('dp', 'seq')), may hold values from -0.109375 to 0.109375
- outer_bias: bfloat16 [768], P(('dp', 'seq')), may hold values from -1.25 to 1.25
- second_gain: bfloat16 [768], P(('dp', 'seq')), may hold values from 0.5 to 1.5
- second_shift: bfloat16 [768], P(('dp', 'seq')), may hold values from -1.25 to 1.25
- cotangent: float32 [32, 1024, 768], P('dp', 'seq'), may hold values from -6 to 6
Outputs:
- layer_output: float32 [32, 1024, 768], P('dp', 'seq')
- input_grad: float32 [32, 1024, 768], P('dp', 'seq')
- query_weight_grad: float32 [768, 768], P(('dp', 'seq'))
- query_bias_grad: float32 [768], P(('dp', 'seq'))
- key_weight_grad: float32 [768, 768], P(('dp', 'seq'))
- value_weight_grad: float32 [768, 768], P(('dp', 'seq'))
- value_bias_grad: float32 [768], P(('dp', 'seq'))
- output_weight_grad: float32 [768, 768], P(('dp', 'seq'))
- output_bias_grad: float32 [768], P(('dp', 'seq'))
- first_gain_grad: float32 [768], P(('dp', 'seq'))
- first_shift_grad: float32 [768], P(('dp', 'seq'))
- inner_weight_grad: float32 [768, 3072], P(('dp', 'seq'))
- inner_bias_grad: float32 [3072], P(('dp', 'seq'))
- outer_weight_grad: float32 [3072, 768], P(('dp', 'seq'))
- outer_bias_grad: float32 [768], P(('dp', 'seq'))
- second_gain_grad: float32 [768], P(('dp', 'seq'))
- second_shift_grad: float32 [768], P(('dp', 'seq'))
The draws below stay inside these ranges and needn't reach their ends.
Inputs may be any that keep to these rules, and one draw needn't show every extreme that they name: `segments`: in each sequence the segment numbers never fall; each document is a run of 1 to 512 tokens, and one has exactly 512.
All inputs are finite; a program needn't handle non-finite values. No bound on the sum of `padding` on one device may be relied on, other than what follows from the above.
Results may differ from the reference program's by a relative error of at most 0.014.
The reference program's roundings to bfloat16 on the way count: a program that leaves them out, or rounds other values in their place, can miss the bound.
Values may be sent and summed in bfloat16 or wider, within the bound.
A program may use at most 192 MiB of HBM per device.

```python
import math
import jax
import jax.numpy as jnp
import numpy as np
from jax import lax

D = 768
HEADS = 12
HEAD_DIM = 64
FF = 3072
SEQ_LEN = 1024
SEQ_ALL = 32
SEG_COUNT = 4
SEG_MOST = 512


def place_ends(array, key, low, top_value):
    longest = array.shape.index(max(array.shape))
    spots = []
    for shift in (0, 1):
        where = [jax.random.randint(jax.random.fold_in(key, axis), (), 0, length) for axis, length in enumerate(array.shape)]
        where[longest] = (where[longest] + shift) % array.shape[longest]
        spots.append(tuple(where))
    return array.at[spots[0]].set(low).at[spots[1]].set(top_value)


def block_levels(stream_key, extent, split, low, largest):
    level, own = 1.0, jax.random.fold_in(stream_key, 6)
    for axis_at, parts in split:
        heights = jnp.exp(jax.random.uniform(jax.random.fold_in(own, axis_at), (parts,), jnp.float32, low / len(split), largest / len(split)))
        level = level * jnp.repeat(heights, extent[axis_at] // parts).reshape([-1 if axis == axis_at else 1 for axis in range(len(extent))])
    return level


def length_profile(count, total, bound, slope):
    portions = [(1 << 20) // math.isqrt(standing ** slope) + 1 for standing in range(2, count + 1)]
    rest, given = total - bound - (count - 1), [1] * (count - 1)
    while rest > 0:
        movable = [i for i in range(count - 1) if given[i] < bound]
        pool, left = sum([portions[i] for i in movable]), rest
        for i in movable:
            extra = min(bound - given[i], max(1, left * portions[i] // pool), rest)
            given[i] = given[i] + extra
            rest = rest - extra
    return np.array([bound] + given)


def uneven_parts(key, amount, total, limit, skew):
    if amount == 2:
        one = jax.random.randint(key, (), max(1, total - limit), min(limit, total - 1) + 1)
        return jnp.stack([one, total - one])
    tallies = jnp.asarray(length_profile(amount, total, limit, skew), jnp.int32)
    twos = (amount - 1) // 2
    donor, taker = tallies[1:1 + 2 * twos:2], tallies[2:2 + 2 * twos:2]
    room = jnp.minimum(donor - 1, limit - taker)
    passed = jax.random.randint(jax.random.fold_in(key, 1), (twos,), 0, 1 << 20) % (room + 1)
    tallies = tallies.at[1:1 + 2 * twos:2].set(donor - passed).at[2:2 + 2 * twos:2].set(taker + passed)
    return tallies[jax.random.permutation(jax.random.fold_in(key, 2), amount)]


def gaussian(stream_key, shape, scale, bound, cuts=(), kind=jnp.bfloat16):
    drawn = scale * jax.random.normal(stream_key, shape, jnp.float32)
    if cuts:
        drawn = drawn * block_levels(stream_key, shape, cuts, -0.22, 0.18)
    return jnp.clip(drawn, -bound, bound).astype(kind)


def setup_inputs(seed: int = 0) -> dict:
    seeds = jax.random.split(jax.random.key(seed), 20)
    tokens = gaussian(seeds[0], (SEQ_ALL, SEQ_LEN, D), 1.0, 6.0, ((0, 16), (1, 2)), jnp.float32)
    segments = jax.vmap(lambda own: jnp.searchsorted(jnp.cumsum(uneven_parts(own, SEG_COUNT, SEQ_LEN, SEG_MOST, 0)), jnp.arange(SEQ_LEN), side="right"))(jax.random.split(seeds[1], SEQ_ALL)).reshape((SEQ_ALL, SEQ_LEN)).astype(jnp.int32)
    padding = place_ends((jax.random.randint(seeds[2], (SEQ_ALL, SEQ_LEN), 0, 8) < 7).astype(jnp.int32), jax.random.fold_in(seeds[2], 1), 0, 1)
    query_weight = gaussian(seeds[3], (D, D), (D // 2) ** -0.5, 0.3125, ((0, 32),))
    query_bias = gaussian(seeds[4], (D,), 0.2, 1.25, ((0, 32),))
    key_weight = gaussian(seeds[5], (D, D), (D // 2) ** -0.5, 0.3125, ((0, 32),))
    value_weight = gaussian(seeds[6], (D, D), D ** -0.5, 0.21875, ((0, 32),))
    value_bias = gaussian(seeds[7], (D,), 0.2, 1.25, ((0, 32),))
    output_weight = gaussian(seeds[8], (D, D), (D // 16) ** -0.5, 0.875, ((0, 32),))
    output_bias = gaussian(seeds[9], (D,), 0.2, 1.25, ((0, 32),))
    first_gain = jnp.clip(1.0 + 0.1 * jax.random.normal(seeds[10], (D,), jnp.float32), 0.5, 1.5).astype(jnp.bfloat16)
    first_shift = gaussian(seeds[11], (D,), 0.2, 1.25, ((0, 32),))
    inner_weight = gaussian(seeds[12], (D, FF), D ** -0.5, 0.21875, ((0, 32),))
    inner_bias = gaussian(seeds[13], (FF,), 0.2, 1.25, ((0, 32),))
    outer_weight = gaussian(seeds[14], (FF, D), FF ** -0.5, 0.109375, ((0, 32),))
    outer_bias = gaussian(seeds[15], (D,), 0.2, 1.25, ((0, 32),))
    second_gain = jnp.clip(1.0 + 0.1 * jax.random.normal(seeds[16], (D,), jnp.float32), 0.5, 1.5).astype(jnp.bfloat16)
    second_shift = gaussian(seeds[17], (D,), 0.2, 1.25, ((0, 32),))
    cotangent = gaussian(seeds[18], (SEQ_ALL, SEQ_LEN, D), 1.0, 6.0, ((0, 16), (1, 2)), jnp.float32)
    return {"tokens": tokens, "segments": segments, "padding": padding, "query_weight": query_weight, "query_bias": query_bias, "key_weight": key_weight, "value_weight": value_weight, "value_bias": value_bias, "output_weight": output_weight, "output_bias": output_bias, "first_gain": first_gain, "first_shift": first_shift, "inner_weight": inner_weight, "inner_bias": inner_bias, "outer_weight": outer_weight, "outer_bias": outer_bias, "second_gain": second_gain, "second_shift": second_shift, "cotangent": cotangent}


@jax.custom_vjp
def low(v):
    return lax.optimization_barrier(v.astype(jnp.bfloat16)).astype(jnp.float32)

@jax.custom_vjp
def low_back(v):
    return v

def low_keep(v):
    return (low(v), None)

def low_pass(kept, grad):
    return (grad,)

def back_keep(v):
    return (v, None)

def back_low(kept, grad):
    return (low(grad),)
low.defvjp(low_keep, low_pass)
low_back.defvjp(back_keep, back_low)

def matmul(left, right):
    return jnp.dot(left, right, precision=lax.Precision.HIGHEST, preferred_element_type=jnp.float32)

def layer_norm(summed, gain, shift):
    center = summed - lax.optimization_barrier(jnp.mean(summed, axis=-1, keepdims=True))
    spread = lax.optimization_barrier(jnp.mean(center * center, axis=-1, keepdims=True))
    return center * lax.rsqrt(spread + 1e-05) * gain + shift

def attend(queries, keys_all, values_all, segments, padding, index):
    seq_index = index // HEADS
    column = index % HEADS * HEAD_DIM
    anchor = index * 0
    query_part = lax.dynamic_slice(queries, (seq_index, anchor, column), (1, SEQ_LEN, HEAD_DIM))[0]
    key_part = lax.dynamic_slice(keys_all, (seq_index, anchor, column), (1, SEQ_LEN, HEAD_DIM))[0]
    value_part = lax.dynamic_slice(values_all, (seq_index, anchor, column), (1, SEQ_LEN, HEAD_DIM))[0]
    seg_row = lax.dynamic_index_in_dim(segments, seq_index, 0, keepdims=False)
    pad_row = lax.dynamic_index_in_dim(padding, seq_index, 0, keepdims=False)
    allowed = (seg_row[:, None] == seg_row[None, :]) & ((pad_row[None, :] == 1) | (pad_row[:, None] == 0))
    scores = low_back(matmul(query_part, key_part.T) * 0.125)
    scores = jnp.where(allowed, scores, -1e+30)
    probs = jax.nn.softmax(scores, axis=-1)
    return matmul(low(probs), value_part)

def reference(tokens, segments, padding, query_weight, query_bias, key_weight, value_weight, value_bias, output_weight, output_bias, first_gain, first_shift, inner_weight, inner_bias, outer_weight, outer_bias, second_gain, second_shift, cotangent):
    params = (query_weight.astype(jnp.float32), query_bias.astype(jnp.float32), key_weight.astype(jnp.float32), value_weight.astype(jnp.float32), value_bias.astype(jnp.float32), output_weight.astype(jnp.float32), output_bias.astype(jnp.float32), first_gain.astype(jnp.float32), first_shift.astype(jnp.float32), inner_weight.astype(jnp.float32), inner_bias.astype(jnp.float32), outer_weight.astype(jnp.float32), outer_bias.astype(jnp.float32), second_gain.astype(jnp.float32), second_shift.astype(jnp.float32))

    def forward(token_in, weights):
        query_matrix, query_vector, key_matrix, value_matrix, value_vector, output_matrix, output_vector, gain_first, shift_first, inner_matrix, inner_vector, outer_matrix, outer_vector, gain_second, shift_second = weights
        token_rows = token_in.reshape(SEQ_ALL * SEQ_LEN, D)
        token_low = low(token_rows)
        queries = low(low_back(matmul(token_low, query_matrix) + query_vector)).reshape(SEQ_ALL, SEQ_LEN, D)
        keys_all = low(low_back(matmul(token_low, key_matrix))).reshape(SEQ_ALL, SEQ_LEN, D)
        values_all = low(low_back(matmul(token_low, value_matrix) + value_vector)).reshape(SEQ_ALL, SEQ_LEN, D)

        def one_head(index):
            return attend(queries, keys_all, values_all, segments, padding, index)
        mixed = lax.map(jax.checkpoint(one_head), jnp.arange(SEQ_ALL * HEADS, dtype=jnp.int32))
        mixed = mixed.reshape(SEQ_ALL, HEADS, SEQ_LEN, HEAD_DIM).transpose(0, 2, 1, 3).reshape(SEQ_ALL * SEQ_LEN, D)
        mixed = low(low_back(mixed))
        branch = low_back(matmul(mixed, output_matrix) + output_vector)
        hidden = layer_norm(token_rows + branch, gain_first, shift_first)
        inner = low_back(matmul(low(hidden), inner_matrix) + inner_vector)
        activation = low(jax.nn.gelu(inner, approximate=False))
        outer = low_back(matmul(activation, outer_matrix) + outer_vector)
        return layer_norm(hidden + outer, gain_second, shift_second).reshape(SEQ_ALL, SEQ_LEN, D)
    output, pull = jax.vjp(forward, tokens.astype(jnp.float32), params)
    input_grad, grads = pull(cotangent.astype(jnp.float32))
    return (output, input_grad, grads[0], grads[1], grads[2], grads[3], grads[4], grads[5], grads[6], grads[7], grads[8], grads[9], grads[10], grads[11], grads[12], grads[13], grads[14])
```

```python
import functools

import jax
import jax.numpy as jnp
from jax import lax
from jax.experimental import pallas as pl
from jax.experimental.pallas import tpu as pltpu
from jax.sharding import PartitionSpec as P

HEADS = 12
HEAD_DIM = 64


neg_big = -1e30


def matmul(left, right):
    return jnp.dot(left, right, preferred_element_type=jnp.float32)


def transposed_left(left, right):
    return lax.dot_general(
        left, right, (((0,), (0,)), ((), ())), preferred_element_type=jnp.float32
    )


def transposed_right(left, right):
    return lax.dot_general(
        left, right, (((1,), (1,)), ((), ())), preferred_element_type=jnp.float32
    )


def layer_norm(summed, gain, shift):
    center = summed - jnp.mean(summed, axis=-1, keepdims=True)
    spread = jnp.mean(center * center, axis=-1, keepdims=True)
    return center * lax.rsqrt(spread + 1e-05) * gain + shift


def exact_gelu(values):
    return jax.nn.gelu(values, approximate=False)


def gathered_layer(
    tokens,
    segments,
    padding,
    query_weight,
    query_bias,
    key_weight,
    value_weight,
    value_bias,
    output_weight,
    output_bias,
    first_gain,
    first_shift,
    inner_weight,
    inner_bias,
    outer_weight,
    outer_bias,
    second_gain,
    second_shift,
    cotangent,
):
    gathered = (
        lax.all_gather(query_weight, ("dp", "seq"), axis=0, tiled=True),
        lax.all_gather(query_bias, ("dp", "seq"), axis=0, tiled=True),
        lax.all_gather(key_weight, ("dp", "seq"), axis=0, tiled=True),
        lax.all_gather(value_weight, ("dp", "seq"), axis=0, tiled=True),
        lax.all_gather(value_bias, ("dp", "seq"), axis=0, tiled=True),
        lax.all_gather(output_weight, ("dp", "seq"), axis=0, tiled=True),
        lax.all_gather(output_bias, ("dp", "seq"), axis=0, tiled=True),
        lax.all_gather(first_gain, ("dp", "seq"), axis=0, tiled=True),
        lax.all_gather(first_shift, ("dp", "seq"), axis=0, tiled=True),
        lax.all_gather(inner_weight, ("dp", "seq"), axis=0, tiled=True),
        lax.all_gather(inner_bias, ("dp", "seq"), axis=0, tiled=True),
        lax.all_gather(outer_weight, ("dp", "seq"), axis=0, tiled=True),
        lax.all_gather(outer_bias, ("dp", "seq"), axis=0, tiled=True),
        lax.all_gather(second_gain, ("dp", "seq"), axis=0, tiled=True),
        lax.all_gather(second_shift, ("dp", "seq"), axis=0, tiled=True),
    )
    (
        query_matrix,
        query_vector,
        key_matrix,
        value_matrix,
        value_vector,
        output_matrix,
        output_vector,
        gain_first,
        shift_first,
        inner_matrix,
        inner_vector,
        outer_matrix,
        outer_vector,
        gain_second,
        shift_second,
    ) = gathered
    gain_first = gain_first.astype(jnp.float32)
    shift_first = shift_first.astype(jnp.float32)
    gain_second = gain_second.astype(jnp.float32)
    shift_second = shift_second.astype(jnp.float32)
    count_seq, block_len, features = tokens.shape
    offset = lax.axis_index("seq") * block_len
    token_rows = tokens.reshape(count_seq * block_len, features)
    token_low = token_rows.astype(jnp.bfloat16)
    queries = (
        (matmul(token_low, query_matrix) + query_vector.astype(jnp.float32))
        .astype(jnp.bfloat16)
        .reshape(count_seq, block_len, features)
    )
    keys_local = (
        matmul(token_low, key_matrix).astype(jnp.bfloat16).reshape(count_seq, block_len, features)
    )
    values_local = (
        (matmul(token_low, value_matrix) + value_vector.astype(jnp.float32))
        .astype(jnp.bfloat16)
        .reshape(count_seq, block_len, features)
    )
    keys_all, values_all = (
        lax.all_gather(keys_local, "seq", axis=1, tiled=True),
        lax.all_gather(values_local, "seq", axis=1, tiled=True),
    )
    query_segment = lax.dynamic_slice_in_dim(segments, offset, block_len, 1)
    query_padding = lax.dynamic_slice_in_dim(padding, offset, block_len, 1)
    allowed = (query_segment[:, :, None] == segments[:, None, :]) & (
        (padding[:, None, :] == 1) | (query_padding[:, :, None] == 0)
    )

    def head_slices(head_index):
        column = head_index * HEAD_DIM
        query_head = lax.dynamic_slice_in_dim(queries, column, HEAD_DIM, 2)
        key_head = lax.dynamic_slice_in_dim(keys_all, column, HEAD_DIM, 2)
        value_head = lax.dynamic_slice_in_dim(values_all, column, HEAD_DIM, 2)
        scores = (
            jnp.einsum("sqd,skd->sqk", query_head, key_head, preferred_element_type=jnp.float32)
            * 0.125
        )
        scores = jnp.where(allowed, scores, neg_big)
        return (column, query_head, key_head, value_head, scores)

    def forward_head(head_index, carry):
        mixed, logsum = carry
        column, query_head, key_head, value_head, scores = head_slices(head_index)
        row_max = jnp.max(scores, axis=2, keepdims=True)
        exponent = jnp.exp(scores - row_max)
        row_total = jnp.sum(exponent, axis=2, keepdims=True)
        probs_low = (exponent / row_total).astype(jnp.bfloat16)
        head_part = jnp.einsum(
            "sqk,skd->sqd", probs_low, value_head, preferred_element_type=jnp.float32
        ).astype(jnp.bfloat16)
        mixed = lax.dynamic_update_slice_in_dim(mixed, head_part, column, 2)
        logsum = lax.dynamic_update_index_in_dim(
            logsum, (row_max + jnp.log(row_total))[:, :, 0], head_index, 0
        )
        return (mixed, logsum)

    mixed, logsum = lax.fori_loop(
        0,
        HEADS,
        forward_head,
        (
            jnp.zeros((count_seq, block_len, features), jnp.bfloat16),
            jnp.zeros((HEADS, count_seq, block_len), jnp.float32),
        ),
    )
    mixed_rows = mixed.reshape(count_seq * block_len, features)
    first_sum = token_rows + matmul(mixed_rows, output_matrix) + output_vector.astype(jnp.float32)
    hidden, first_pull = jax.vjp(layer_norm, first_sum, gain_first, shift_first)
    hidden_low = hidden.astype(jnp.bfloat16)
    inner = matmul(hidden_low, inner_matrix) + inner_vector.astype(jnp.float32)
    activation, gelu_pull = jax.vjp(exact_gelu, inner)
    activation_low = activation.astype(jnp.bfloat16)
    second_sum = hidden + matmul(activation_low, outer_matrix) + outer_vector.astype(jnp.float32)
    layer_output, second_pull = jax.vjp(layer_norm, second_sum, gain_second, shift_second)
    again = (
        lax.all_gather(query_weight, ("dp", "seq"), axis=0, tiled=True),
        lax.all_gather(key_weight, ("dp", "seq"), axis=0, tiled=True),
        lax.all_gather(value_weight, ("dp", "seq"), axis=0, tiled=True),
        lax.all_gather(output_weight, ("dp", "seq"), axis=0, tiled=True),
        lax.all_gather(inner_weight, ("dp", "seq"), axis=0, tiled=True),
        lax.all_gather(outer_weight, ("dp", "seq"), axis=0, tiled=True),
    )
    again_query, again_key, again_value, again_output, again_inner, again_outer = again
    second_back, second_gains, second_shifts = second_pull(
        cotangent.reshape(count_seq * block_len, features)
    )
    outer_low = second_back.astype(jnp.bfloat16)
    outer_delta = transposed_left(activation_low, outer_low)
    inner_back = gelu_pull(transposed_right(outer_low, again_outer))[0].astype(jnp.bfloat16)
    inner_delta = transposed_left(hidden_low, inner_back)
    hidden_back = transposed_right(inner_back, again_inner) + second_back
    first_back, first_gains, first_shifts = first_pull(hidden_back)
    branch_low = first_back.astype(jnp.bfloat16)
    output_delta = transposed_left(mixed_rows, branch_low)
    mixed_back = (
        transposed_right(branch_low, again_output)
        .astype(jnp.bfloat16)
        .reshape(count_seq, block_len, features)
    )
    total_len = segments.shape[1]

    def backward_head(head_index, carry):
        query_acc, key_acc, value_acc = carry
        column, query_head, key_head, value_head, scores = head_slices(head_index)
        grad_head = lax.dynamic_slice_in_dim(mixed_back, column, HEAD_DIM, 2)
        row_log = lax.dynamic_index_in_dim(logsum, head_index, 0, keepdims=False)
        probs = jnp.exp(scores - row_log[:, :, None])
        value_part = jnp.einsum(
            "sqk,sqd->skd",
            probs.astype(jnp.bfloat16),
            grad_head,
            preferred_element_type=jnp.float32,
        )
        prob_back = jnp.einsum(
            "sqd,skd->sqk", grad_head, value_head, preferred_element_type=jnp.float32
        )
        score_back = (
            probs * (prob_back - jnp.sum(probs * prob_back, axis=2, keepdims=True))
        ).astype(jnp.bfloat16)
        query_part = (
            jnp.einsum("sqk,skd->sqd", score_back, key_head, preferred_element_type=jnp.float32)
            * 0.125
        )
        key_part = (
            jnp.einsum("sqk,sqd->skd", score_back, query_head, preferred_element_type=jnp.float32)
            * 0.125
        )
        query_acc = lax.dynamic_update_slice_in_dim(query_acc, query_part, column, 2)
        key_acc = lax.dynamic_update_slice_in_dim(key_acc, key_part, column, 2)
        value_acc = lax.dynamic_update_slice_in_dim(value_acc, value_part, column, 2)
        return (query_acc, key_acc, value_acc)

    query_acc, key_acc, value_acc = lax.fori_loop(
        0,
        HEADS,
        backward_head,
        (
            jnp.zeros((count_seq, block_len, features), jnp.float32),
            jnp.zeros((count_seq, total_len, features), jnp.float32),
            jnp.zeros((count_seq, total_len, features), jnp.float32),
        ),
    )
    key_sum, value_sum = (
        lax.psum_scatter(
            key_acc.astype(jnp.bfloat16), "seq", scatter_dimension=1, tiled=True
        ).astype(jnp.float32),
        lax.psum_scatter(
            value_acc.astype(jnp.bfloat16), "seq", scatter_dimension=1, tiled=True
        ).astype(jnp.float32),
    )
    query_low = query_acc.reshape(count_seq * block_len, features).astype(jnp.bfloat16)
    key_low = key_sum.reshape(count_seq * block_len, features).astype(jnp.bfloat16)
    value_low = value_sum.reshape(count_seq * block_len, features).astype(jnp.bfloat16)
    query_delta = transposed_left(token_low, query_low)
    key_delta = transposed_left(token_low, key_low)
    value_delta = transposed_left(token_low, value_low)
    input_back = (
        transposed_right(query_low, again_query)
        + transposed_right(key_low, again_key)
        + transposed_right(value_low, again_value)
        + first_back
    )
    shards = (
        lax.psum_scatter(query_delta, ("dp", "seq"), scatter_dimension=0, tiled=True),
        lax.psum_scatter(
            jnp.sum(query_low.astype(jnp.float32), axis=0),
            ("dp", "seq"),
            scatter_dimension=0,
            tiled=True,
        ),
        lax.psum_scatter(key_delta, ("dp", "seq"), scatter_dimension=0, tiled=True),
        lax.psum_scatter(value_delta, ("dp", "seq"), scatter_dimension=0, tiled=True),
        lax.psum_scatter(
            jnp.sum(value_low.astype(jnp.float32), axis=0),
            ("dp", "seq"),
            scatter_dimension=0,
            tiled=True,
        ),
        lax.psum_scatter(output_delta, ("dp", "seq"), scatter_dimension=0, tiled=True),
        lax.psum_scatter(
            jnp.sum(branch_low.astype(jnp.float32), axis=0),
            ("dp", "seq"),
            scatter_dimension=0,
            tiled=True,
        ),
        lax.psum_scatter(first_gains, ("dp", "seq"), scatter_dimension=0, tiled=True),
        lax.psum_scatter(first_shifts, ("dp", "seq"), scatter_dimension=0, tiled=True),
        lax.psum_scatter(inner_delta, ("dp", "seq"), scatter_dimension=0, tiled=True),
        lax.psum_scatter(
            jnp.sum(inner_back.astype(jnp.float32), axis=0),
            ("dp", "seq"),
            scatter_dimension=0,
            tiled=True,
        ),
        lax.psum_scatter(outer_delta, ("dp", "seq"), scatter_dimension=0, tiled=True),
        lax.psum_scatter(
            jnp.sum(outer_low.astype(jnp.float32), axis=0),
            ("dp", "seq"),
            scatter_dimension=0,
            tiled=True,
        ),
        lax.psum_scatter(second_gains, ("dp", "seq"), scatter_dimension=0, tiled=True),
        lax.psum_scatter(second_shifts, ("dp", "seq"), scatter_dimension=0, tiled=True),
    )
    return (
        layer_output.reshape(tokens.shape),
        input_back.reshape(tokens.shape),
        shards[0],
        shards[1],
        shards[2],
        shards[3],
        shards[4],
        shards[5],
        shards[6],
        shards[7],
        shards[8],
        shards[9],
        shards[10],
        shards[11],
        shards[12],
        shards[13],
        shards[14],
    )


MESH = pl.DeviceIdType.MESH
BF = jnp.bfloat16
F32 = jnp.float32
LOG2E = 1.4426950408889634
SCORE_SCALE = 0.125 * LOG2E
VMEM_MOST = 66 * 1024 * 1000
BLOCK = 256


def grid_dims(mesh):
    return (mesh.shape["dp"] // 4, 2, 2, mesh.shape["seq"])


def swappable(mesh, shape):
    count, rows, features = shape
    return (
        mesh.shape["seq"] == 2
        and count == 2
        and mesh.shape["dp"] % 4 == 0
        and rows % (2 * BLOCK) == 0
        and features % 128 == 0
    )


class Place:
    def __init__(self, dims):
        self.dims = dims
        nz, nx, nc, ny = dims
        dp, y = lax.axis_index("dp"), lax.axis_index("seq")
        z, x, c = dp // (nx * nc), (dp // nc) % nx, dp % nc
        self.z, self.x, self.c, self.y = z, x, c, y
        self.xo, self.co, self.yo = 1 - x, 1 - c, 1 - y
        self.along_z = [self.device(lax.rem(z + d, nz), x, c, y) for d in range(1, nz)]
        self.along_x = self.device(z, self.xo, c, y)
        self.along_c = self.device(z, x, self.co, y)
        self.along_y = self.device(z, x, c, self.yo)

    def device(self, z, x, c, y):
        nz, nx, nc, ny = self.dims
        return ((z * nx + x) * nc + c, y)

    def greet(self):
        barrier = pltpu.get_barrier_semaphore()
        self.partners = self.along_z + [self.along_x, self.along_c, self.along_y]
        for partner in self.partners:
            pl.semaphore_signal(barrier, inc=1, device_id=partner, device_id_type=MESH)

    def meet(self):
        pl.semaphore_wait(pltpu.get_barrier_semaphore(), len(self.partners))


def remote(src, dst, send, recv, device):
    return pltpu.make_async_remote_copy(
        src_ref=src, dst_ref=dst, send_sem=send, recv_sem=recv, device_id=device, device_id_type=MESH
    )


def halves(width):
    part = width // 256 * 128
    return pl.ds(0, part), pl.ds(part, width - part)


def gather_kernel(dims, count, *refs):
    nz = dims[0]
    ins, (tokens, cotangent) = refs[:count], refs[count : count + 2]
    outs, (low_out, cot_out) = refs[count + 2 : 2 * count + 2], refs[2 * count + 2 : 2 * count + 4]
    own_t, other_t, other_c, low, low_c = refs[2 * count + 4 : 2 * count + 9]
    local, zs, zr, ps, pr, qs, qr, cs, cr, ts, tr = refs[2 * count + 9 :]
    at = Place(dims)
    z, x, c, y = at.z, at.x, at.c, at.y
    loads = [
        pltpu.make_async_copy(tokens.at[at.yo], other_t, local.at[count]),
        pltpu.make_async_copy(tokens.at[y], own_t, local.at[count + 1]),
        pltpu.make_async_copy(cotangent.at[at.yo], other_c, local.at[count + 2]),
    ]
    for load in loads:
        load.start()
    at.greet()
    loads[0].wait()
    low[1] = other_t[...].astype(BF)
    at.meet()
    own, along = [], []
    for i in range(count):
        copy = pltpu.make_async_copy(ins[i], outs[i].at[z, x, c, y], local.at[i])
        copy.start()
        own.append(copy)
        row = []
        for d in range(1, nz):
            k = remote(ins[i], outs[i].at[z, x, c, y], zs.at[i, d - 1], zr.at[i, d - 1], at.along_z[d - 1])
            k.start()
            row.append(k)
        along.append(row)
    swap = remote(low.at[1], low_out.at[1], ts.at[0], tr.at[0], at.along_y)
    swap.start()
    loads[1].wait()
    low[0] = own_t[...].astype(BF)
    loads[2].wait()
    low_c[...] = other_c[...].astype(BF)
    keep = pltpu.make_async_copy(low.at[0], low_out.at[0], local.at[count + 3])
    keep.start()
    second, third, fourth = [None] * count, [None] * count, [None] * count

    def spread(i):
        own[i].wait()
        for k in along[i]:
            k.wait()
        a, b = halves(ins[i].shape[1])
        a, b = outs[i].at[:, x, c, y, :, a], outs[i].at[:, x, c, y, :, b]
        second[i] = (
            remote(a, a, ps.at[i, 0], pr.at[i, 0], at.along_x),
            remote(b, b, ps.at[i, 1], pr.at[i, 1], at.along_y),
        )
        for k in second[i]:
            k.start()

    def spread_again(i):
        for k in second[i]:
            k.wait()
        a, b = halves(ins[i].shape[1])
        a, b = outs[i].at[:, :, c, y, :, a], outs[i].at[:, x, c, :, :, b]
        third[i] = (
            remote(a, a, qs.at[i, 0], qr.at[i, 0], at.along_y),
            remote(b, b, qs.at[i, 1], qr.at[i, 1], at.along_x),
        )
        for k in third[i]:
            k.start()

    def share(i):
        for k in third[i]:
            k.wait()
        a = outs[i].at[:, :, c]
        fourth[i] = remote(a, a, cs.at[i], cr.at[i], at.along_c)
        fourth[i].start()

    swap_c = remote(low_c, cot_out, ts.at[1], tr.at[1], at.along_y)
    for t in range(count + 2):
        if t < count:
            spread(t)
        if 0 <= t - 1 < count:
            spread_again(t - 1)
        if t == count - 1:
            swap_c.start()
        if 0 <= t - 2 < count:
            share(t - 2)
    for k in fourth:
        k.wait()
    swap.wait()
    swap_c.wait()
    keep.wait()


def gather(dims, shards, tokens, cotangent):
    nz = dims[0]
    n = len(shards)
    rows, d = tokens.shape[1:]
    hbm, vmem = pl.BlockSpec(memory_space=pl.ANY), pl.BlockSpec(memory_space=pltpu.VMEM)
    sem = pltpu.SemaphoreType.DMA
    out = [jax.ShapeDtypeStruct(dims + s.shape, s.dtype) for s in shards]
    out += [jax.ShapeDtypeStruct((2, rows, d), BF), jax.ShapeDtypeStruct((rows, d), BF)]
    return pl.pallas_call(
        functools.partial(gather_kernel, dims, n),
        out_shape=out,
        in_specs=[vmem] * n + [hbm] * 2,
        out_specs=[hbm] * (n + 2),
        scratch_shapes=[pltpu.VMEM((rows, d), F32)] * 3
        + [pltpu.VMEM((2, rows, d), BF), pltpu.VMEM((rows, d), BF)]
        + [sem((n + 4,)), sem((n, nz - 1)), sem((n, nz - 1))]
        + [sem((n, 2))] * 4
        + [sem((n,))] * 2
        + [sem((2,))] * 2,
        compiler_params=pltpu.CompilerParams(collective_id=0, has_side_effects=True),
        name="gather",
    )(*shards, tokens, cotangent)


def scatter_kernel(dims, count, *refs):
    nz, nx, nc, ny = dims
    ins, vec, swaps = refs[:count], refs[count], refs[count + 1 : count + 3]
    outs, vec_out = refs[count + 3 : 2 * count + 3], refs[2 * count + 3]
    swap_outs = refs[2 * count + 4 : 2 * count + 6]
    rest = list(refs[2 * count + 6 :])
    m0, r0, r1, r2, r3 = (rest[k * count : (k + 1) * count] for k in range(5))
    vm, vc, vx, vy, vz = rest[5 * count : 5 * count + 5]
    local, s0, q0, s1, q1, s2, q2, s3, q3, vs, vq, ws, wq = rest[5 * count + 5 :]
    at = Place(dims)
    z, x, c, y = at.z, at.x, at.c, at.y
    at.greet()
    loads = []
    for i in range(count):
        k = pltpu.make_async_copy(ins[i].at[:, :, c], m0[i], local.at[i])
        k.start()
        loads.append(k)
    at.meet()
    v0 = remote(vec, vc, vs.at[0], vq.at[0], at.along_c)
    v0.start()
    c0 = []
    for i in range(count):
        k = remote(ins[i].at[:, :, at.co], r0[i], s0.at[i], q0.at[i], at.along_c)
        k.start()
        c0.append(k)
    back = [remote(swaps[j], swap_outs[j], ws.at[j], wq.at[j], at.along_y) for j in range(2)]
    back[0].start()
    c1, c2, c3 = [None] * count, [None] * count, [None] * count

    def add(dst, src):
        dst[...] = (dst[...].astype(F32) + src[...].astype(F32)).astype(dst.dtype)

    def first(i):
        loads[i].wait()
        c0[i].wait()
        a, b = halves(ins[i].shape[-1])

        def body(t, _):
            add(m0[i].at[t // nx, t % nx], r0[i].at[t // nx, t % nx])
            return 0

        lax.fori_loop(0, nz * nx, body, 0)
        c1[i] = (
            remote(m0[i].at[:, :, at.yo, :, a], r1[i].at[0], s1.at[i, 0], q1.at[i, 0], at.along_y),
            remote(m0[i].at[:, at.xo, :, :, b], r1[i].at[1], s1.at[i, 1], q1.at[i, 1], at.along_x),
        )
        for k in c1[i]:
            k.start()

    def second(i):
        for k in c1[i]:
            k.wait()
        a, b = halves(ins[i].shape[-1])

        def body(t, _):
            u, v = t // nx, t % nx
            add(m0[i].at[u, v, y, :, a], r1[i].at[0, u, v])
            add(m0[i].at[u, x, v, :, b], r1[i].at[1, u, v])
            return 0

        lax.fori_loop(0, nz * nx, body, 0)
        c2[i] = (
            remote(m0[i].at[:, at.xo, y, :, a], r2[i].at[0], s2.at[i, 0], q2.at[i, 0], at.along_x),
            remote(m0[i].at[:, x, at.yo, :, b], r2[i].at[1], s2.at[i, 1], q2.at[i, 1], at.along_y),
        )
        for k in c2[i]:
            k.start()

    def third(i):
        for k in c2[i]:
            k.wait()
        a, b = halves(ins[i].shape[-1])

        def body(u, _):
            add(m0[i].at[u, x, y, :, a], r2[i].at[0, u])
            add(m0[i].at[u, x, y, :, b], r2[i].at[1, u])
            return 0

        lax.fori_loop(0, nz, body, 0)
        c3[i] = []
        for d in range(1, nz):
            k = remote(
                m0[i].at[lax.rem(z + d, nz), x, y], r3[i].at[d - 1], s3.at[i, d - 1], q3.at[i, d - 1], at.along_z[d - 1]
            )
            k.start()
            c3[i].append(k)

    def fourth(i):
        for k in c3[i]:
            k.wait()
        total = m0[i][z, x, y].astype(F32)
        for d in range(1, nz):
            total = total + r3[i][d - 1].astype(F32)
        outs[i][...] = total

    for t in range(count + 3):
        if t < count:
            first(t)
        if t == 0:
            v0.wait()
            vm[...] = vec[...] + vc[...]
            v1 = remote(vm, vx, vs.at[1], vq.at[1], at.along_x)
            v1.start()
            back[1].start()
        if 0 <= t - 1 < count:
            second(t - 1)
        if t == 1:
            v1.wait()
            vm[...] = vm[...] + vx[...]
            v2 = remote(vm, vy, vs.at[2], vq.at[2], at.along_y)
            v2.start()
        if 0 <= t - 2 < count:
            third(t - 2)
        if t == 2:
            v2.wait()
            vm[...] = vm[...] + vy[...]
            v3 = [remote(vm, vz.at[d], vs.at[3 + d], vq.at[3 + d], at.along_z[d]) for d in range(nz - 1)]
            for k in v3:
                k.start()
        if 0 <= t - 3 < count:
            fourth(t - 3)
    for k in v3:
        k.wait()
    total = vm[...]
    for d in range(nz - 1):
        total = total + vz[d]
    vec_out[...] = total
    for k in back:
        k.wait()


def scatter(dims, grads, vec, swaps):
    nz, nx, nc, ny = dims
    n = len(grads)
    hbm, vmem = pl.BlockSpec(memory_space=pl.ANY), pl.BlockSpec(memory_space=pltpu.VMEM)
    shapes = [g.shape[4:] for g in grads]
    struct, sem, space = jax.ShapeDtypeStruct, pltpu.SemaphoreType.DMA, pltpu.VMEM
    out = [struct(s, F32) for s in shapes] + [struct(vec.shape, F32)] + [struct(a.shape, a.dtype) for a in swaps]
    scratch = (
        [space((nz, nx, ny) + s, BF) for s in shapes] * 2
        + [space((2, nz, nx, s[0], s[1] // 2), BF) for s in shapes]
        + [space((2, nz, s[0], s[1] // 2), BF) for s in shapes]
        + [space((nz - 1,) + s, BF) for s in shapes]
        + [space(vec.shape, F32)] * 4
        + [space((nz - 1,) + vec.shape, F32)]
        + [sem((n,))] * 3
        + [sem((n, 2))] * 4
        + [sem((n, nz - 1))] * 2
        + [sem((nz + 2,))] * 2
        + [sem((2,))] * 2
    )
    return pl.pallas_call(
        functools.partial(scatter_kernel, dims, n),
        out_shape=out,
        in_specs=[hbm] * n + [vmem] + [hbm] * 2,
        out_specs=[vmem] * (n + 1) + [hbm] * 2,
        scratch_shapes=scratch,
        compiler_params=pltpu.CompilerParams(collective_id=1, has_side_effects=True, vmem_limit_bytes=VMEM_MOST),
        name="scatter",
    )(*grads, vec, *swaps)


def lanes(shape):
    return lax.broadcasted_iota(jnp.int32, shape, len(shape) - 1)


def features(segments, padding):
    lane = jnp.arange(128, dtype=jnp.int32)[None, :] % HEAD_DIM
    same = segments[:, None] == lane
    real = padding[:, None] == 1
    query = jnp.where(lane < 56, same, (lane == 56) & real).astype(BF)
    hidden = jnp.where(lane < 56, ~same, (lane == 56) & ~real)
    key = jnp.where(hidden, neg_big, jnp.where((lane > 56) & (lane < 60), 1.0, 0.0)).astype(BF)
    return query, key


def pieces(value):
    high = value.astype(BF).astype(F32)
    value = value - high
    middle = value.astype(BF).astype(F32)
    return high, middle, value - middle


def attend_kernel(tok, wq, wk, wv, bq, bv, fq, fk, q_o, k_o, v_o, mixed_o, lse_o):
    n, d = tok.shape

    def project(i, _):
        r = pl.ds(i * BLOCK, BLOCK)
        t = tok[r, :]
        q_o[r, :] = (matmul(t, wq[...]) + bq[...]).astype(BF)
        k_o[r, :] = matmul(t, wk[...]).astype(BF)
        v_o[r, :] = (matmul(t, wv[...]) + bv[...]).astype(BF)
        return 0

    lax.fori_loop(0, n // BLOCK, project, 0)
    lse_o[...] = jnp.zeros_like(lse_o)

    def pair(p, _):
        cols = pl.ds(pl.multiple_of(p * 128, 128), 128)
        kp, vp, f = k_o[:, cols], v_o[:, cols], fk[...]
        low = lanes((n, 128)) < HEAD_DIM
        zero = jnp.zeros_like(vp)
        ks = (jnp.where(low, kp, f), jnp.where(low, f, kp))
        vs = (jnp.where(low, vp, zero), jnp.where(low, zero, vp))
        lane = lanes((BLOCK, 128))
        low = lane < HEAD_DIM
        for b in range(n // BLOCK):
            r = pl.ds(b * BLOCK, BLOCK)
            qp, f = q_o[r, cols], fq[r, :]
            qs = (jnp.where(low, qp, f), jnp.where(low, f, qp))
            out, lse = None, lse_o[r, :]
            for h in range(2):
                s = transposed_right(qs[h], ks[h])
                top = jnp.max(s, axis=1, keepdims=True)
                e = jnp.exp2((s - top) * SCORE_SCALE)
                total = jnp.sum(e, axis=1, keepdims=True)
                o = matmul(e.astype(BF), vs[h]) * (1.0 / total)
                out = o if out is None else out + o
                lse = jnp.where(lane == 2 * p + h, top + 8.0 * jnp.log(total), lse)
            mixed_o[r, cols] = out.astype(BF)
            lse_o[r, :] = lse
        return 0

    lax.fori_loop(0, d // 128, pair, 0)


def attend(tok, wq, wk, wv, bq, bv, fq, fk):
    n, d = tok.shape
    vmem = pl.BlockSpec(memory_space=pltpu.VMEM)
    return pl.pallas_call(
        attend_kernel,
        out_shape=[jax.ShapeDtypeStruct((n, d), BF)] * 4 + [jax.ShapeDtypeStruct((n, 128), F32)],
        in_specs=[vmem] * 8,
        out_specs=[vmem] * 5,
        compiler_params=pltpu.CompilerParams(vmem_limit_bytes=VMEM_MOST),
        name="attend",
    )(tok, wq, wk, wv, bq, bv, fq, fk)


def attend_back_kernel(
    tok, wq, wk, wv, q_r, k_r, v_r, mixed, do_r, lse_r, fq, fk, first_back,
    own_o, other_o, dwq_o, dwk_o, dwv_o, dbq_o, dbv_o, dq_s, dk_s, dv_s, p_s, ds_s,
):
    n, d = tok.shape

    def pair(p, _):
        cols = pl.ds(pl.multiple_of(p * 128, 128), 128)
        kp, vp, qp, op, dp = (ref[:, cols] for ref in (k_r, v_r, q_r, mixed, do_r))
        lane = lanes((n, 128))
        low, slot = lane < HEAD_DIM, lane % HEAD_DIM
        fkv, fqv, lse = fk[...], fq[...].astype(F32), lse_r[...]
        ones = jnp.where((slot > 56) & (slot < 60), 1.0, 0.0).astype(BF)
        zero = jnp.zeros_like(vp)
        prod = dp.astype(F32) * op.astype(F32)
        dk = dv = dq = None
        for h in range(2):
            mine = low if h == 0 else jnp.logical_not(low)
            a, b, c = pieces(-jnp.sum(jnp.where(lane == 2 * p + h, lse, 0.0), axis=1, keepdims=True))
            f = jnp.where(slot == 57, a, jnp.where(slot == 58, b, jnp.where(slot == 59, c, fqv))).astype(BF)
            a, b, c = pieces(-jnp.sum(jnp.where(mine, prod, 0.0), axis=1, keepdims=True))
            g = jnp.where(slot == 57, a, jnp.where(slot == 58, b, jnp.where(slot == 59, c, 0.0))).astype(BF)
            qx, kx = jnp.where(mine, qp, f), jnp.where(mine, kp, fkv)
            dox, vx = jnp.where(mine, dp, g), jnp.where(mine, vp, ones)
            q0, k0, do0 = (jnp.where(mine, v, zero) for v in (qp, kp, dp))
            for kb in range(n // BLOCK):
                r = slice(kb * BLOCK, (kb + 1) * BLOCK)
                e = jnp.exp2(transposed_right(kx[r], qx) * SCORE_SCALE)
                t = transposed_right(vx[r], dox)
                p_s[r, :] = e.astype(BF)
                ds_s[r, :] = (e * t).astype(BF)
            parts = (matmul(p_s[...], do0), matmul(ds_s[...], q0), transposed_left(ds_s[...], k0))
            dv, dk, dq = parts if dv is None else (dv + parts[0], dk + parts[1], dq + parts[2])
        dq_s[:, cols] = (dq * 0.125).astype(BF)
        dk_s[:, cols] = (dk * 0.125).astype(BF)
        dv_s[:, cols] = dv.astype(BF)
        return 0

    lax.fori_loop(0, d // 128, pair, 0)
    dbq_o[...] = jnp.sum(dq_s[...].astype(F32), axis=0, keepdims=True)
    dbv_o[...] = jnp.sum(dv_s[...].astype(F32), axis=0, keepdims=True)
    t = tok[...]
    dwq_o[...] = transposed_left(t, dq_s[...]).astype(BF)
    dwk_o[...] = transposed_left(t, dk_s[...]).astype(BF)
    dwv_o[...] = transposed_left(t, dv_s[...]).astype(BF)

    def tail(i, shift, out):
        r, w = pl.ds(shift + i * BLOCK, BLOCK), pl.ds(i * BLOCK, BLOCK)
        total = (
            transposed_right(dq_s[r, :], wq[...])
            + transposed_right(dk_s[r, :], wk[...])
            + transposed_right(dv_s[r, :], wv[...])
            + first_back[r, :]
        )
        out[w, :] = total.astype(out.dtype)
        return 0

    lax.fori_loop(0, n // 2 // BLOCK, lambda i, _: tail(i, 0, own_o), 0)
    lax.fori_loop(0, n // 2 // BLOCK, lambda i, _: tail(i, n // 2, other_o), 0)


def attend_back(tok, wq, wk, wv, q, k, v, mixed, do, lse, fq, fk, first_back):
    n, d = tok.shape
    vmem, struct = pl.BlockSpec(memory_space=pltpu.VMEM), jax.ShapeDtypeStruct
    return pl.pallas_call(
        attend_back_kernel,
        out_shape=[struct((n // 2, d), F32), struct((n // 2, d), BF)]
        + [struct((d, d), BF)] * 3
        + [struct((1, d), F32)] * 2,
        in_specs=[vmem] * 13,
        out_specs=[vmem] * 7,
        scratch_shapes=[pltpu.VMEM((n, d), BF)] * 3 + [pltpu.VMEM((n, n), BF)] * 2,
        compiler_params=pltpu.CompilerParams(vmem_limit_bytes=VMEM_MOST),
        name="attend_back",
    )(tok, wq, wk, wv, q, k, v, mixed, do, lse, fq, fk, first_back)


def row_mean(value):
    return jnp.mean(value, axis=1, keepdims=True)


def column_sum(value):
    return jnp.sum(value, axis=0, keepdims=True)


def middle_kernel(
    place, tok, low, mixed, cot, cot_low, wp, wi, wo, bp, g1, s1, bi, bo, g2, s2,
    own_o, other_o, first_o, back_o, dwo_o, dwi_o, dwp_o, vec_o, dbi_o,
    act_s, ib_s, slope_s, hl_s, ol_s, br_s, mx_s, *, steps,
):
    i = pl.program_id(0)
    wide, part = wi.shape[1], dwo_o.shape[0]

    @pl.when(i < steps)
    def _():
        r = pl.ds(pl.multiple_of(i * BLOCK, BLOCK), BLOCK)

        @pl.when(i == 0)
        def _():
            vec_o[...] = jnp.zeros_like(vec_o)
            dbi_o[...] = jnp.zeros_like(dbi_o)

        is_own = i < steps // 2
        mx = mixed[...]
        mx_s[r, :] = mx
        first_sum = jnp.where(is_own, tok[0], low[0].astype(F32)) + matmul(mx, wp[...]) + bp[...]
        center = first_sum - row_mean(first_sum)
        scale1 = lax.rsqrt(row_mean(center * center) + 1e-05)
        n1 = center * scale1
        hidden = n1 * g1[...] + s1[...]
        hl = hidden.astype(BF)
        hl_s[r, :] = hl
        for j in range(wide // part):
            c = slice(j * part, (j + 1) * part)
            v = matmul(hl, wi[:, c]) + bi[:, c]
            phi = 0.5 + 0.5 * lax.erf(v * 0.7071067811865476)
            act_s[r, c] = (v * phi).astype(BF)
            slope_s[:, c] = phi + v * (jnp.exp2(v * v * (-0.5 * LOG2E)) * 0.3989422804014327)
        second_sum = hidden + matmul(act_s[r, :], wo[...]) + bo[...]
        center = second_sum - row_mean(second_sum)
        scale2 = lax.rsqrt(row_mean(center * center) + 1e-05)
        n2 = center * scale2
        result = n2 * g2[...] + s2[...]

        @pl.when(is_own)
        def _():
            own_o[...] = result

        @pl.when(jnp.logical_not(is_own))
        def _():
            other_o[...] = result.astype(BF)

        ct = jnp.where(is_own, cot[0], cot_low[...].astype(F32))
        cg = ct * g2[...]
        second_back = (cg - row_mean(cg) - n2 * row_mean(cg * n2)) * scale2
        ol = second_back.astype(BF)
        ol_s[r, :] = ol
        for j in range(wide // part):
            c = slice(j * part, (j + 1) * part)
            ib = (transposed_right(ol, wo[c, :]) * slope_s[:, c]).astype(BF)
            ib_s[r, c] = ib
            dbi_o[:, c] += column_sum(ib.astype(F32))
        hidden_back = transposed_right(ib_s[r, :], wi[...]) + second_back
        cg = hidden_back * g1[...]
        first_back = (cg - row_mean(cg) - n1 * row_mean(cg * n1)) * scale1
        first_o[...] = first_back
        br = first_back.astype(BF)
        br_s[r, :] = br
        back_o[...] = transposed_right(br, wp[...]).astype(BF)
        sums = (ct * n2, ct, ol.astype(F32), hidden_back * n1, hidden_back, br.astype(F32))
        for k, value in enumerate(sums):
            vec_o[k : k + 1, :] += column_sum(value)

    @pl.when(i >= steps)
    def _():
        j = i - steps
        c = pl.ds(pl.multiple_of(j * part, part), part)
        dwo_o[...] = transposed_left(act_s[:, c], ol_s[...]).astype(BF)
        dwi_o[...] = transposed_left(hl_s[...], ib_s[:, c]).astype(BF)

        @pl.when(j == 0)
        def _():
            dwp_o[...] = transposed_left(mx_s[...], br_s[...]).astype(BF)


def middle(place, tok, low, mixed, cot, cot_low, wp, wi, wo, bp, g1, s1, bi, bo, g2, s2):
    n, d = mixed.shape
    ff = wi.shape[1]
    steps, part = n // BLOCK, min(ff, 768)
    half, more = steps // 2, ff // part
    struct, clip = jax.ShapeDtypeStruct, jnp.clip
    own = lambda i, y: (y[0], clip(i, 0, half - 1), 0)
    row = lambda i, y: (clip(i, 0, steps - 1), 0)
    first, last = (lambda i, y: (clip(i, 0, half - 1), 0)), (lambda i, y: (clip(i - half, 0, half - 1), 0))
    tile = lambda i: jnp.maximum(i - steps, 0)
    full = lambda a: pl.BlockSpec(a.shape, lambda i, y: (0,) * a.ndim, pipeline_mode=pl.Buffered(1))
    block = lambda index: pl.BlockSpec((BLOCK, d), index)
    still = lambda i, y: (0, 0)
    vecs = [bp, g1, s1, bi, bo, g2, s2]
    return pl.pallas_call(
        functools.partial(middle_kernel, steps=steps),
        grid_spec=pltpu.PrefetchScalarGridSpec(
            num_scalar_prefetch=1,
            grid=(steps + more,),
            in_specs=[
                pl.BlockSpec((1, BLOCK, d), own),
                pl.BlockSpec((1, BLOCK, d), lambda i, y: (1, clip(i - half, 0, half - 1), 0)),
                block(row),
                pl.BlockSpec((1, BLOCK, d), own),
                block(last),
            ]
            + [full(w) for w in (wp, wi, wo)]
            + [full(v) for v in vecs],
            out_specs=[
                block(first),
                block(last),
                block(row),
                block(row),
                pl.BlockSpec((part, d), lambda i, y: (tile(i), 0)),
                pl.BlockSpec((d, part), lambda i, y: (0, tile(i))),
                pl.BlockSpec((d, d), still),
                pl.BlockSpec((8, d), still),
                pl.BlockSpec((1, ff), still),
            ],
            scratch_shapes=[pltpu.VMEM((n, ff), BF)] * 2
            + [pltpu.VMEM((BLOCK, ff), F32)]
            + [pltpu.VMEM((n, d), BF)] * 4,
        ),
        out_shape=[struct((n // 2, d), F32), struct((n // 2, d), BF), struct((n, d), F32), struct((n, d), BF)]
        + [struct((ff, d), BF), struct((d, ff), BF), struct((d, d), BF), struct((8, d), F32), struct((1, ff), F32)],
        compiler_params=pltpu.CompilerParams(vmem_limit_bytes=VMEM_MOST, dimension_semantics=("arbitrary",)),
        name="middle",
    )(place, tok, low, mixed, cot, cot_low, wp, wi, wo, *vecs)


def swapped_layer(
    mesh, tokens, segments, padding, query_weight, query_bias, key_weight, value_weight, value_bias,
    output_weight, output_bias, first_gain, first_shift, inner_weight, inner_bias, outer_weight,
    outer_bias, second_gain, second_shift, cotangent,
):
    dims = grid_dims(mesh)
    parts = dims[0] * dims[1] * dims[2] * dims[3]
    y = lax.axis_index("seq")
    mine = lax.axis_index("dp") * 2 + y
    count, rows, d = tokens.shape
    small = [query_bias, value_bias, output_bias, first_gain, first_shift, outer_bias, second_gain, second_shift]
    width = d // parts
    strip = jnp.concatenate(small + [inner_bias]).astype(F32)
    size = -(-strip.shape[0] // 128) * 128
    strip = jnp.broadcast_to(jnp.pad(strip, (0, size - strip.shape[0]))[None], (8, size))
    weights = [query_weight, key_weight, value_weight, output_weight, inner_weight, outer_weight]
    got = gather(dims, [strip] + weights, tokens, cotangent)
    table = got[0].reshape(parts, 8, size)[:, 0]
    wq, wk, wv, wp, wi, wo = (g.reshape(-1, g.shape[-1]) for g in got[1:7])
    low, cot_low = got[7], got[8]
    vectors = table[:, : 8 * width].reshape(parts, 8, width).transpose(1, 0, 2).reshape(8, d)
    bq, bv, bp, g1, s1, bo, g2, s2 = (vectors[k : k + 1] for k in range(8))
    bi = table[:, 8 * width : 8 * width + inner_bias.shape[0]].reshape(1, -1)

    def in_order(array):
        line = lax.dynamic_index_in_dim(array, y, 0, keepdims=False).reshape(2, rows)
        return jnp.where(y == 0, line, line[::-1]).reshape(-1)

    fq, fk = features(in_order(segments), in_order(padding))
    tok = low.reshape(2 * rows, d)
    q, k, v, mixed, lse = attend(tok, wq, wk, wv, bq, bv, fq, fk)
    out_own, out_other, first_back, do, dwo, dwi, dwp, vec, dbi = middle(
        y.reshape(1), tokens, low, mixed, cotangent, cot_low, wp, wi, wo, bp, g1, s1, bi, bo, g2, s2
    )
    in_own, in_other, dwq, dwk, dwv, dbq, dbv = attend_back(
        tok, wq, wk, wv, q, k, v, mixed, do, lse, fq, fk, first_back
    )
    sums = jnp.concatenate([vec[:6], dbq, dbv, dbi.reshape(-1, d)])
    sums = jnp.pad(sums, ((0, -sums.shape[0] % 8), (0, 0)))
    grads = [g.reshape(dims + (g.shape[0] // parts, g.shape[1])) for g in (dwo, dwi, dwp, dwq, dwk, dwv)]
    dwo, dwi, dwp, dwq, dwk, dwv, sums, out_got, in_got = scatter(dims, grads, sums, [out_other, in_other])
    own = lax.dynamic_slice(sums, (0, mine * width), (8, width))
    dg2, ds2, dbo, dg1, ds1, dbp, dbq, dbv = (own[k] for k in range(8))
    inner_width = inner_bias.shape[0]
    dbi = lax.dynamic_slice(sums[8 : 8 + inner_width * parts // d].reshape(-1), (mine * inner_width,), (inner_width,))

    def whole(own, got):
        got = got.astype(F32)
        return jnp.where(y == 0, jnp.stack([own, got]), jnp.stack([got, own]))

    return (
        whole(out_own, out_got), whole(in_own, in_got), dwq, dbq, dwk, dwv, dbv, dwp, dbp, dg1, ds1,
        dwi, dbi, dwo, dbo, dg2, ds2,
    )


def solution(mesh):
    placed = (
        P("dp", "seq", None),
        P("dp", None),
        P("dp", None),
        P(("dp", "seq"), None),
        P(("dp", "seq")),
        P(("dp", "seq"), None),
        P(("dp", "seq"), None),
        P(("dp", "seq")),
        P(("dp", "seq"), None),
        P(("dp", "seq")),
        P(("dp", "seq")),
        P(("dp", "seq")),
        P(("dp", "seq"), None),
        P(("dp", "seq")),
        P(("dp", "seq"), None),
        P(("dp", "seq")),
        P(("dp", "seq")),
        P(("dp", "seq")),
        P("dp", "seq", None),
    )
    def layer(*args):
        if swappable(mesh, args[0].shape):
            return swapped_layer(mesh, *args)
        return gathered_layer(*args)

    return jax.shard_map(
        layer,
        mesh=mesh,
        in_specs=placed,
        out_specs=(
            P("dp", "seq", None),
            P("dp", "seq", None),
            P(("dp", "seq"), None),
            P(("dp", "seq")),
            P(("dp", "seq"), None),
            P(("dp", "seq"), None),
            P(("dp", "seq")),
            P(("dp", "seq"), None),
            P(("dp", "seq")),
            P(("dp", "seq")),
            P(("dp", "seq")),
            P(("dp", "seq"), None),
            P(("dp", "seq")),
            P(("dp", "seq"), None),
            P(("dp", "seq")),
            P(("dp", "seq")),
            P(("dp", "seq")),
        ),
        check_vma=False,
    )
```
